32 devices in a mesh: pipe: 4 (over x, core), expert: 8 (over z, y).
Axes of the slice: x: 2, y: 2, z: 4, core: 2. Of those that a mesh axis runs over, the one named last changes fastest.
Arguments:
- tokens: bfloat16 [1024, 6144], P('expert'), may hold values from -6 to 6
- expert_ids: int32 [1024, 2], P('expert'), may hold values from 0 to 7, as said below
- gate_weight: bfloat16 [6144, 16384], P(None, 'expert'), may hold values from -0.078125 to 0.078125
- up_weight: bfloat16 [6144, 16384], P(None, 'expert'), may hold values from -0.078125 to 0.078125
- d_hidden: bfloat16 [256, 16384], P('pipe', 'expert'), may hold values from -6 to 6
Outputs:
- hidden: bfloat16 [256, 16384], P('pipe', 'expert')
- d_tokens: float32 [1024, 6144], P('expert', 'pipe')
The draws below stay inside these ranges and needn't reach their ends.
Inputs may be any that keep to these rules, and one draw needn't show every extreme that they name: `expert_ids`: the two ids of a token differ. Among the 128 tokens of one block at least 8 and at most 32 name expert 0, and in every draw some block has exactly 32 such tokens.
All inputs are finite; a program needn't handle non-finite values.
Results may differ from the reference program's by a relative error of at most 0.0029.
Values may be sent and summed in bfloat16 or wider, within the bound.
A program may use at most 128 MiB of HBM per device.

```python
import jax
import jax.numpy as jnp
from jax import lax

D = 6144
FF = 16384
EXPERTS = 8
TOPK = 2
TOK_DEV = 128
CAP = 32
SPAN = 8
TOKENS = 1024
ROWS = 256
N_PIPE = 4
N_EXPERT = 8


def draw_expert_ids(key, part):
    blocks = TOKENS // TOK_DEV
    key_list = jax.random.split(jax.random.fold_in(key, 17), 6)
    counts = jax.random.randint(key_list[0], (blocks,), CAP // 4, CAP + 1)
    full_block = jax.random.randint(key_list[1], (), 0, blocks)
    counts = jnp.where(jnp.arange(blocks) == full_block, CAP, counts)
    scores = jax.random.randint(key_list[2], (blocks, TOK_DEV), 0, 1 << 20) * TOK_DEV + jnp.arange(TOK_DEV)
    token_rank = jnp.argsort(jnp.argsort(scores, axis=1), axis=1)
    chosen = token_rank < counts[:, None]
    lead_id = jax.random.randint(key_list[3], (blocks, TOK_DEV), 1, EXPERTS)
    offset = jax.random.randint(key_list[4], (blocks, TOK_DEV), 1, EXPERTS - 1)
    second = 1 + (lead_id - 1 + offset) % (EXPERTS - 1)
    lead_id = jnp.where(chosen, 0, lead_id)
    swapped = jax.random.randint(key_list[5], (blocks, TOK_DEV), 0, 2) == 1
    column_one = jnp.where(swapped, second, lead_id)
    column_two = jnp.where(swapped, lead_id, second)
    return jnp.stack([column_one, column_two], axis=2).reshape(TOKENS, TOPK).astype(jnp.int32)


def steps_of(key, shape, pieces, smallest, largest):
    loudness, own = 1.0, jax.random.fold_in(key, 6)
    for position, shards_of in pieces:
        steps = jnp.exp(jax.random.uniform(jax.random.fold_in(own, position), (shards_of,), jnp.float32, smallest / len(pieces), largest / len(pieces)))
        loudness = loudness * jnp.repeat(steps, shape[position] // shards_of).reshape([-1 if axis == position else 1 for axis in range(len(shape))])
    return loudness


def bell_draw(key, extent, spread, bound, pieces=(), kind=jnp.bfloat16):
    values = spread * jax.random.normal(key, extent, jnp.float32)
    if pieces:
        values = values * steps_of(key, extent, pieces, -0.22, 0.18)
    return jnp.clip(values, -bound, bound).astype(kind)


def setup_inputs(seed: int = 0) -> dict:
    key_of = jax.random.split(jax.random.key(seed), 6)
    return {
        "tokens": bell_draw(key_of[0], (TOKENS, D), 1.0, 6.0, ((0, 8),)),
        "expert_ids": draw_expert_ids(jax.random.fold_in(key_of[5], 71), 0),
        "gate_weight": bell_draw(key_of[2], (D, FF), D ** -0.5, 0.078125, ((1, 8),)),
        "up_weight": bell_draw(key_of[3], (D, FF), D ** -0.5, 0.078125, ((1, 8),)),
        "d_hidden": bell_draw(key_of[4], (ROWS, FF), 1.0, 6.0, ((0, 4), (1, 8))),
    }


def reference(tokens, expert_ids, gate_weight, up_weight, d_hidden):
    blocks = N_EXPERT
    is_named = jnp.any(expert_ids == 0, axis=1).astype(jnp.int32).reshape(blocks, TOK_DEV)
    slot_before = jnp.cumsum(is_named, axis=1) - is_named
    positions = jnp.arange(CAP, dtype=jnp.int32)
    select = ((is_named[:, :, None] == 1) & (slot_before[:, :, None] == positions)).astype(jnp.float32)
    inputs = tokens.reshape(blocks, TOK_DEV, D).astype(jnp.float32)
    routed = jnp.einsum("etc,etd->ecd", select, inputs, precision=lax.Precision.HIGHEST).astype(jnp.bfloat16)
    routed = routed.reshape(blocks, N_PIPE, SPAN, D).transpose(1, 0, 2, 3).reshape(N_PIPE, blocks * SPAN, D)
    upstream_all = d_hidden.reshape(N_PIPE, blocks * SPAN, FF)

    def one_group(index):
        rows_in = lax.dynamic_index_in_dim(routed, index, 0, keepdims=False)
        upstream = lax.dynamic_index_in_dim(upstream_all, index, 0, keepdims=False).astype(jnp.float32)
        gate_value = jnp.dot(rows_in, gate_weight, preferred_element_type=jnp.float32)
        up_value = jnp.dot(rows_in, up_weight, preferred_element_type=jnp.float32)
        sigmoid_gate = jax.nn.sigmoid(gate_value)
        activated = gate_value * sigmoid_gate
        hidden_part = (activated * up_value).astype(jnp.bfloat16)
        d_gate = (upstream * up_value * sigmoid_gate * (1.0 + gate_value * (1.0 - sigmoid_gate))).astype(jnp.bfloat16)
        d_up = (upstream * activated).astype(jnp.bfloat16)
        d_rows = jnp.dot(d_gate, gate_weight.T, preferred_element_type=jnp.float32)
        d_rows = d_rows + jnp.dot(d_up, up_weight.T, preferred_element_type=jnp.float32)
        return hidden_part, d_rows

    hidden, d_parts = lax.map(one_group, jnp.arange(N_PIPE, dtype=jnp.int32))
    d_slots = d_parts.reshape(N_PIPE, blocks, SPAN, D).transpose(1, 0, 2, 3).reshape(blocks, CAP, D)
    d_tokens = jnp.einsum("etc,ecd->etd", select, d_slots, precision=lax.Precision.HIGHEST)
    return hidden.reshape(ROWS, FF), d_tokens.reshape(TOKENS, D)
```

```python
import functools

import jax
import jax.numpy as jnp
from jax import lax
from jax.experimental import pallas as pl
from jax.experimental.pallas import tpu as pltpu
from jax.sharding import PartitionSpec as P

CAP = 32
CORES = 2
UNIT = 16
STEPS = 4
MESH_ID = pl.DeviceIdType.MESH


def slot_select(expert_ids, first_slot, slot_count):
    is_named = jnp.any(expert_ids == 0, axis=1).astype(jnp.int32)
    slot_before = jnp.cumsum(is_named) - is_named
    positions = first_slot + jnp.arange(slot_count, dtype=jnp.int32)
    marked = (is_named[:, None] == 1) & (slot_before[:, None] == positions[None, :])
    return marked.astype(jnp.float32)


def plain_body(tokens, expert_ids, gate_weight, up_weight, d_hidden):
    hidden_units = gate_weight.shape[1]
    slot_span = CAP // lax.axis_size("pipe")
    own_select = slot_select(expert_ids, lax.axis_index("pipe") * slot_span, slot_span)
    routed = jnp.einsum(
        "tj,td->jd", own_select.astype(jnp.bfloat16), tokens, preferred_element_type=jnp.float32
    ).astype(jnp.bfloat16)
    piece = lax.all_gather(routed, "expert", axis=0, tiled=True)
    gate_part = jnp.dot(piece, gate_weight, preferred_element_type=jnp.float32)
    up_part = jnp.dot(piece, up_weight, preferred_element_type=jnp.float32)
    joined = jnp.concatenate([gate_part, up_part], axis=1)
    gate_value = joined[:, :hidden_units]
    up_value = joined[:, hidden_units:]
    sigmoid_gate = jax.nn.sigmoid(gate_value)
    activated = gate_value * sigmoid_gate
    hidden = (activated * up_value).astype(jnp.bfloat16)
    upstream = d_hidden.astype(jnp.float32)
    d_gate = (
        upstream * up_value * sigmoid_gate * (1.0 + gate_value * (1.0 - sigmoid_gate))
    ).astype(jnp.bfloat16)
    d_up = (upstream * activated).astype(jnp.bfloat16)
    result = jnp.einsum("nh,dh->nd", d_gate, gate_weight, preferred_element_type=jnp.float32)
    slot_grads = lax.psum_scatter(
        result + jnp.einsum("nh,dh->nd", d_up, up_weight, preferred_element_type=jnp.float32),
        "expert",
        scatter_dimension=0,
        tiled=True,
    )
    pieces = lax.all_to_all(slot_grads, "pipe", split_axis=1, concat_axis=0, tiled=True)
    full_select = slot_select(expert_ids, 0, CAP)
    d_tokens = jnp.einsum("tc,cd->td", full_select, pieces, precision=lax.Precision.HIGHEST)
    return (hidden, d_tokens)


def expert_kernel(nz, ny, tok, ids, gate, up, dh, hid, dtok,
                  tokv, own, oth, wg, wu, accg, accu, dhv, dgv, duv, hst,
                  csend, crecv, full, keep, ysend, yrecv, zsend, zrecv, fin, xsend, xrecv,
                  load_sem, send_sem, recv_sem):
    pipe, expert = lax.axis_index("pipe"), lax.axis_index("expert")
    x, c = pipe // CORES, lax.rem(pipe, CORES)
    z, y = expert // ny, lax.rem(expert, ny)
    half_steps = STEPS // 2
    width = tokv.shape[2]
    half = wg.shape[3]
    count = tok.shape[0]
    span = width * half_steps
    ring = range(1, nz)
    z_to = {d: lax.rem(z + d, nz) for d in ring}
    z_from = {d: lax.rem(z + nz - d, nz) for d in ring}
    core_peer = (x * CORES + 1 - c, expert)
    x_peer = ((1 - x) * CORES + c, expert)
    y_peer = (pipe, z * ny + 1 - y)
    z_peer = {d: (pipe, z_to[d] * ny + y) for d in ring}

    taken = [0, 0]

    def load(src, dst):
        taken[0] += 1
        copy = pltpu.make_async_copy(src, dst, load_sem.at[taken[0] - 1])
        copy.start()
        return copy

    def send(src, dst, device):
        taken[1] += 1
        index = taken[1] - 1
        copy = pltpu.make_async_remote_copy(
            src_ref=src, dst_ref=dst, send_sem=send_sem.at[index], recv_sem=recv_sem.at[index],
            device_id=device, device_id_type=MESH_ID)
        copy.start()
        sent.append(copy)
        return copy

    sent = []

    def offset(other, s):
        part = c if other == 0 else 1 - c
        where = 1 - x if s < half_steps else x
        return pl.multiple_of((where * CORES + part) * span + (s % half_steps) * width, 128)

    barrier = pltpu.get_barrier_semaphore()
    peers = [core_peer, x_peer, y_peer] + [z_peer[d] for d in ring]
    for peer in peers:
        pl.semaphore_signal(barrier, inc=1, device_id=peer, device_id_type=MESH_ID)

    mine = pl.ds(pl.multiple_of(c * half, 128), half)
    others = pl.ds(pl.multiple_of((1 - c) * half, 128), half)
    tok_loads = [load(tok.at[:, pl.ds(offset(0, s), width)], tokv.at[s]) for s in range(STEPS)]
    w_loads = {}
    for s in range(STEPS):
        for other in (0, 1):
            rows = pl.ds(offset(other, s), width)
            w_loads[other, s] = (
                load(gate.at[rows, mine], wg.at[other, s]), load(up.at[rows, mine], wu.at[other, s]))
    dh_load = load(dh.at[:, mine], dhv.at[c])

    named_col = jnp.where((ids[:, 0:1] == 0) | (ids[:, 1:2] == 0), 1.0, 0.0)
    row_id = lax.broadcasted_iota(jnp.int32, (count, count), 0)
    col_id = lax.broadcasted_iota(jnp.int32, (count, count), 1)
    spread = jnp.broadcast_to(named_col, (count, count))
    before_row = jnp.sum(jnp.where(row_id < col_id, spread, 0.0), axis=0, keepdims=True)
    named_row = jnp.sum(jnp.where(row_id == col_id, spread, 0.0), axis=0, keepdims=True)
    slot_id = (lax.broadcasted_iota(jnp.int32, (UNIT, count), 0) + x * UNIT).astype(jnp.float32)
    select = jnp.where((before_row == slot_id) & (named_row == 1.0), 1.0, 0.0).astype(jnp.bfloat16)

    pl.semaphore_wait(barrier, len(peers))
    dh_copy = send(dh.at[:, others], dhv.at[c], core_peer)

    z_copies, y_copies, core_copies = {}, {}, {}
    for s in range(STEPS):
        tok_loads[s].wait()
        own[s, expert] = jnp.dot(
            select, tokv[s], preferred_element_type=jnp.float32).astype(jnp.bfloat16)
        for d in ring:
            z_copies[s, d] = send(own.at[s, expert], own.at[s, expert], z_peer[d])
        y_copies[s, 0] = send(own.at[s, expert], own.at[s, expert], y_peer)

    def forward(other, s):
        block = (own if other == 0 else oth)[s].reshape(nz * ny * UNIT, width)
        for copy in w_loads[other, s]:
            copy.wait()
        for acc, weight in ((accg, wg), (accu, wu)):
            term = jnp.dot(block, weight[other, s], preferred_element_type=jnp.float32)
            if other == 0 and s == 0:
                acc[...] = term
            else:
                acc[...] += term

    for i in range(STEPS + 2):
        if i < STEPS:
            for d in ring:
                z_copies[i, d].wait_recv()
                place = z_from[d] * ny + y
                y_copies[i, d] = send(own.at[i, place], own.at[i, place], y_peer)
        s = i - 1
        if 0 <= s < STEPS:
            for d in range(nz):
                y_copies[s, d].wait_recv()
            core_copies[s] = send(own.at[s], oth.at[s], core_peer)
            forward(0, s)
        s = i - 2
        if 0 <= s < STEPS:
            core_copies[s].wait_recv()
            forward(1, s)

    dh_load.wait()
    dh_copy.wait_recv()
    blocks = nz * ny
    tile = 256 if half % 256 == 0 else half
    for n in range(0, half, tile):
        cols = slice(n, n + tile)
        gate_value, up_value = accg[:, cols], accu[:, cols]
        first = dhv[0, :, cols].astype(jnp.float32).reshape(blocks, UNIT // 2, tile)
        second = dhv[1, :, cols].astype(jnp.float32).reshape(blocks, UNIT // 2, tile)
        upstream = jnp.stack([first, second], axis=1).reshape(blocks * UNIT, tile)
        sigmoid_gate = jax.nn.sigmoid(gate_value)
        activated = gate_value * sigmoid_gate
        hidden = (activated * up_value).reshape(blocks, 2, UNIT // 2, tile)
        for q in (0, 1):
            hst[q, :, cols] = hidden[:, q].reshape(blocks * UNIT // 2, tile).astype(jnp.bfloat16)
        dgv[:, cols] = (
            upstream * up_value * sigmoid_gate * (1.0 + gate_value * (1.0 - sigmoid_gate))
        ).astype(jnp.bfloat16)
        duv[:, cols] = (upstream * activated).astype(jnp.bfloat16)
    hid_load = load(hst.at[c], hid.at[:, mine])

    contract = (((1,), (1,)), ((), ()))

    def backward(other, s):
        return lax.dot_general(
            dgv[...], wg[other, s], contract, preferred_element_type=jnp.float32
        ) + lax.dot_general(
            duv[...], wu[other, s], contract, preferred_element_type=jnp.float32)

    core_sums, y_sums, z_sums, x_sums = {}, {}, {}, {}
    hid_copy = None
    for i in range(STEPS + 3):
        if i < STEPS:
            csend[i] = backward(1, i).astype(jnp.bfloat16)
            core_sums[i] = send(csend.at[i], crecv.at[i], core_peer)
            full[i % 2] = backward(0, i).reshape(blocks, UNIT, width)
        s = i - 1
        if 0 <= s < STEPS:
            core_sums[s].wait_recv()
            total = crecv[s].astype(jnp.float32).reshape(blocks, UNIT, width)
            full[s % 2] = full[s % 2] + total
            for k in range(nz):
                ysend[s, k] = full[s % 2, k * ny + 1 - y].astype(jnp.bfloat16)
                keep[s, k] = full[s % 2, k * ny + y]
            y_sums[s] = send(ysend.at[s], yrecv.at[s], y_peer)
            if hid_copy is None:
                hid_copy = send(hst.at[1 - c], hid.at[:, mine], core_peer)
        s = i - 2
        if 0 <= s < STEPS:
            y_sums[s].wait_recv()
            for d in ring:
                zsend[s, d - 1] = (
                    keep[s, z_to[d]] + yrecv[s, z_to[d]].astype(jnp.float32)).astype(jnp.bfloat16)
                z_sums[s, d] = send(zsend.at[s, d - 1], zrecv.at[s, d - 1], z_peer[d])
            fin[s] = keep[s, z] + yrecv[s, z].astype(jnp.float32)
        s = i - 3
        if 0 <= s < STEPS:
            for d in ring:
                z_sums[s, d].wait_recv()
            done = fin[s]
            for d in ring:
                done = done + zrecv[s, d - 1].astype(jnp.float32)
            if s < half_steps:
                xsend[s] = done
                x_sums[s] = send(xsend.at[s], xrecv.at[s], x_peer)
            else:
                fin[s] = done

    lane_sum = functools.partial(jnp.sum, axis=1, keepdims=True)
    before_col = lane_sum(jnp.where(col_id < row_id, jnp.broadcast_to(named_row, (count, count)), 0.0))
    lane = lax.broadcasted_iota(jnp.int32, (count, 2 * UNIT), 1)
    position = jnp.where(lane < UNIT, lane + x * UNIT, lane - UNIT + (1 - x) * UNIT)
    placed = jnp.where(
        (before_col == position.astype(jnp.float32)) & (named_col == 1.0), 1.0, 0.0)
    for s in range(half_steps):
        x_sums[s].wait_recv()
        slots = jnp.concatenate([fin[half_steps + s], xrecv[s]], axis=0)
        dtok[:, s * width:(s + 1) * width] = jnp.dot(
            placed, slots, precision=lax.Precision.HIGHEST, preferred_element_type=jnp.float32)

    hid_load.wait()
    hid_copy.wait_recv()
    for copy in sent:
        copy.wait_send()


def fused_body(nz, ny, tokens, expert_ids, gate_weight, up_weight, d_hidden):
    count, features = tokens.shape
    hidden_units = gate_weight.shape[1]
    rows = d_hidden.shape[0]
    width = features // (CORES * STEPS)
    half = hidden_units // CORES
    blocks = nz * ny
    half_steps = STEPS // 2
    bf, f32 = jnp.bfloat16, jnp.float32
    loads = STEPS * 5 + 2
    sends = 2 + STEPS * (nz - 1 + nz + 1) + STEPS * (2 + nz - 1) + half_steps
    hbm = pl.BlockSpec(memory_space=pl.ANY)
    vmem = pl.BlockSpec(memory_space=pltpu.VMEM)
    flops = 8 * blocks * UNIT * features * half
    hidden, d_tokens = pl.pallas_call(
        functools.partial(expert_kernel, nz, ny),
        out_shape=(
            jax.ShapeDtypeStruct((rows, hidden_units), bf),
            jax.ShapeDtypeStruct((count, half_steps * width), f32),
        ),
        in_specs=[hbm, vmem, hbm, hbm, hbm],
        out_specs=(hbm, vmem),
        scratch_shapes=[
            pltpu.VMEM((STEPS, count, width), bf),
            pltpu.VMEM((STEPS, blocks, UNIT, width), bf),
            pltpu.VMEM((STEPS, blocks, UNIT, width), bf),
            pltpu.VMEM((2, STEPS, width, half), bf),
            pltpu.VMEM((2, STEPS, width, half), bf),
            pltpu.VMEM((blocks * UNIT, half), f32),
            pltpu.VMEM((blocks * UNIT, half), f32),
            pltpu.VMEM((2, rows, half), bf),
            pltpu.VMEM((blocks * UNIT, half), bf),
            pltpu.VMEM((blocks * UNIT, half), bf),
            pltpu.VMEM((2, rows, half), bf),
            pltpu.VMEM((STEPS, blocks * UNIT, width), bf),
            pltpu.VMEM((STEPS, blocks * UNIT, width), bf),
            pltpu.VMEM((2, blocks, UNIT, width), f32),
            pltpu.VMEM((STEPS, nz, UNIT, width), f32),
            pltpu.VMEM((STEPS, nz, UNIT, width), bf),
            pltpu.VMEM((STEPS, nz, UNIT, width), bf),
            pltpu.VMEM((STEPS, nz - 1, UNIT, width), bf),
            pltpu.VMEM((STEPS, nz - 1, UNIT, width), bf),
            pltpu.VMEM((STEPS, UNIT, width), f32),
            pltpu.VMEM((half_steps, UNIT, width), f32),
            pltpu.VMEM((half_steps, UNIT, width), f32),
            pltpu.SemaphoreType.DMA((loads,)),
            pltpu.SemaphoreType.DMA((sends,)),
            pltpu.SemaphoreType.DMA((sends,)),
        ],
        compiler_params=pltpu.CompilerParams(
            collective_id=0, has_side_effects=True, vmem_limit_bytes=56 * 1024 * 1024),
        cost_estimate=pl.CostEstimate(
            flops=flops, bytes_accessed=4 * features * half, transcendentals=0),
    )(tokens, expert_ids, gate_weight, up_weight, d_hidden)
    return hidden, d_tokens


def split_of(mesh):
    line = mesh.devices.reshape(mesh.shape["pipe"], mesh.shape["expert"])[0]
    coords = [getattr(device, "coords", None) for device in line]
    if coords[0] is None:
        return len(line) // 2, 2
    ny = len({tuple(at)[1] for at in coords})
    return len(line) // ny, ny


def solution(mesh):
    in_specs = (
        P("expert", None),
        P("expert", None),
        P(None, "expert"),
        P(None, "expert"),
        P("pipe", "expert"),
    )
    out_specs = (P("pipe", "expert"), P("expert", "pipe"))
    nz, ny = split_of(mesh)
    fits = ny == 2 and nz > 1 and mesh.shape["pipe"] == 2 * CORES and 2 * UNIT == CAP
    body = functools.partial(fused_body, nz, ny) if fits else plain_body
    return jax.shard_map(body, mesh=mesh, in_specs=in_specs, out_specs=out_specs, check_vma=False)
```

```python
import functools

import jax
import jax.numpy as jnp
from jax import lax
from jax.experimental import pallas as pl
from jax.experimental.pallas import tpu as pltpu
from jax.sharding import PartitionSpec as P

CAP = 32
CORES = 2
UNIT = 16
STEPS = 6
Y_LAG, C_LAG = 2, 3
ADD_LAG, Y_SUM_LAG, Z_SUM_LAG = 1, 3, 5
MESH_ID = pl.DeviceIdType.MESH


def slot_select(expert_ids, first_slot, slot_count):
    is_named = jnp.any(expert_ids == 0, axis=1).astype(jnp.int32)
    slot_before = jnp.cumsum(is_named) - is_named
    positions = first_slot + jnp.arange(slot_count, dtype=jnp.int32)
    marked = (is_named[:, None] == 1) & (slot_before[:, None] == positions[None, :])
    return marked.astype(jnp.float32)


def plain_body(tokens, expert_ids, gate_weight, up_weight, d_hidden):
    hidden_units = gate_weight.shape[1]
    slot_span = CAP // lax.axis_size("pipe")
    own_select = slot_select(expert_ids, lax.axis_index("pipe") * slot_span, slot_span)
    routed = jnp.einsum(
        "tj,td->jd", own_select.astype(jnp.bfloat16), tokens, preferred_element_type=jnp.float32
    ).astype(jnp.bfloat16)
    piece = lax.all_gather(routed, "expert", axis=0, tiled=True)
    gate_part = jnp.dot(piece, gate_weight, preferred_element_type=jnp.float32)
    up_part = jnp.dot(piece, up_weight, preferred_element_type=jnp.float32)
    joined = jnp.concatenate([gate_part, up_part], axis=1)
    gate_value = joined[:, :hidden_units]
    up_value = joined[:, hidden_units:]
    sigmoid_gate = jax.nn.sigmoid(gate_value)
    activated = gate_value * sigmoid_gate
    hidden = (activated * up_value).astype(jnp.bfloat16)
    upstream = d_hidden.astype(jnp.float32)
    d_gate = (
        upstream * up_value * sigmoid_gate * (1.0 + gate_value * (1.0 - sigmoid_gate))
    ).astype(jnp.bfloat16)
    d_up = (upstream * activated).astype(jnp.bfloat16)
    result = jnp.einsum("nh,dh->nd", d_gate, gate_weight, preferred_element_type=jnp.float32)
    slot_grads = lax.psum_scatter(
        result + jnp.einsum("nh,dh->nd", d_up, up_weight, preferred_element_type=jnp.float32),
        "expert",
        scatter_dimension=0,
        tiled=True,
    )
    pieces = lax.all_to_all(slot_grads, "pipe", split_axis=1, concat_axis=0, tiled=True)
    full_select = slot_select(expert_ids, 0, CAP)
    d_tokens = jnp.einsum("tc,cd->td", full_select, pieces, precision=lax.Precision.HIGHEST)
    return (hidden, d_tokens)


def named_counts(ids, count):
    row_id = lax.broadcasted_iota(jnp.int32, (count, count), 0)
    col_id = lax.broadcasted_iota(jnp.int32, (count, count), 1)
    named_row = jnp.where((ids[0:1, :] == 0) | (ids[1:2, :] == 0), 1.0, 0.0)
    across = jnp.broadcast_to(named_row, (count, count))
    named_col = jnp.sum(jnp.where(row_id == col_id, across, 0.0), axis=1, keepdims=True)
    before_col = jnp.sum(jnp.where(col_id < row_id, across, 0.0), axis=1, keepdims=True)
    down = jnp.broadcast_to(named_col, (count, count))
    before_row = jnp.sum(jnp.where(row_id < col_id, down, 0.0), axis=0, keepdims=True)
    return named_row, before_row, named_col, before_col


def place_kernel(ids, slots, hid_in, dtok, hid_out):
    count = dtok.shape[0]
    hid_out[...] = hid_in[...]
    _, _, named_col, before_col = named_counts(ids, count)
    lane = lax.broadcasted_iota(jnp.int32, (count, 2 * UNIT), 1).astype(jnp.float32)
    placed = jnp.where((before_col == lane) & (named_col == 1.0), 1.0, 0.0)
    dtok[...] = jnp.dot(
        placed, slots[...].reshape(2 * UNIT, dtok.shape[1]),
        precision=lax.Precision.HIGHEST, preferred_element_type=jnp.float32)


def expert_kernel(nz, ny, tok, ids, gate, up, dh, hid, slots,
                  tokv, own, oth, wg, wu, accg, accu, dhv, dgv, duv, hst,
                  csend, crecv, full, keep, ysend, yrecv, zsend, zrecv, fin, xsend, xrecv,
                  load_sem, send_sem, recv_sem):
    pipe, expert = lax.axis_index("pipe"), lax.axis_index("expert")
    x, c = pipe // CORES, lax.rem(pipe, CORES)
    z, y = expert // ny, lax.rem(expert, ny)
    half_steps = STEPS // 2
    width = tokv.shape[2]
    half = wg.shape[3]
    count = tok.shape[0]
    span = width * half_steps
    ring = range(1, nz)
    z_to = {d: lax.rem(z + d, nz) for d in ring}
    z_from = {d: lax.rem(z + nz - d, nz) for d in ring}
    core_peer = (x * CORES + 1 - c, expert)
    x_peer = ((1 - x) * CORES + c, expert)
    y_peer = (pipe, z * ny + 1 - y)
    z_peer = {d: (pipe, z_to[d] * ny + y) for d in ring}

    taken = [0, 0]

    def load(src, dst):
        taken[0] += 1
        copy = pltpu.make_async_copy(src, dst, load_sem.at[taken[0] - 1])
        copy.start()
        return copy

    def send(src, dst, device):
        taken[1] += 1
        index = taken[1] - 1
        copy = pltpu.make_async_remote_copy(
            src_ref=src, dst_ref=dst, send_sem=send_sem.at[index], recv_sem=recv_sem.at[index],
            device_id=device, device_id_type=MESH_ID)
        copy.start()
        sent.append(copy)
        return copy

    sent = []

    def offset(other, s):
        part = c if other == 0 else 1 - c
        where = 1 - x if s < half_steps else x
        return pl.multiple_of((where * CORES + part) * span + (s % half_steps) * width, 128)

    barrier = pltpu.get_barrier_semaphore()
    peers = [core_peer, x_peer, y_peer] + [z_peer[d] for d in ring]
    for peer in peers:
        pl.semaphore_signal(barrier, inc=1, device_id=peer, device_id_type=MESH_ID)

    mine = pl.ds(pl.multiple_of(c * half, 128), half)
    others = pl.ds(pl.multiple_of((1 - c) * half, 128), half)
    tok_loads = [load(tok.at[:, pl.ds(offset(0, s), width)], tokv.at[s]) for s in range(STEPS)]
    w_loads = {}
    for s in range(STEPS):
        for other in (0, 1):
            rows = pl.ds(offset(other, s), width)
            w_loads[other, s] = (
                load(gate.at[rows, mine], wg.at[other, s]), load(up.at[rows, mine], wu.at[other, s]))
    dh_load = load(dh.at[:, mine], dhv.at[c])

    named_row, before_row, _, _ = named_counts(ids, count)
    slot_id = (lax.broadcasted_iota(jnp.int32, (UNIT, count), 0) + x * UNIT).astype(jnp.float32)
    select = jnp.where((before_row == slot_id) & (named_row == 1.0), 1.0, 0.0).astype(jnp.bfloat16)

    pl.semaphore_wait(barrier, len(peers))
    dh_copy = send(dh.at[:, others], dhv.at[c], core_peer)

    z_copies, y_copies, core_copies = {}, {}, {}
    for s in range(STEPS):
        tok_loads[s].wait()
        own[s, expert] = jnp.dot(
            select, tokv[s], preferred_element_type=jnp.float32).astype(jnp.bfloat16)
        for d in ring:
            z_copies[s, d] = send(own.at[s, expert], own.at[s, expert], z_peer[d])
        y_copies[s, 0] = send(own.at[s, expert], own.at[s, expert], y_peer)

    def forward(other, s):
        block = (own if other == 0 else oth)[s].reshape(nz * ny * UNIT, width)
        for copy in w_loads[other, s]:
            copy.wait()
        for acc, weight in ((accg, wg), (accu, wu)):
            term = jnp.dot(block, weight[other, s], preferred_element_type=jnp.float32)
            if other == 0 and s == 0:
                acc[...] = term
            else:
                acc[...] += term

    for i in range(STEPS + C_LAG):
        if i < STEPS:
            for d in ring:
                z_copies[i, d].wait_recv()
                place = z_from[d] * ny + y
                y_copies[i, d] = send(own.at[i, place], own.at[i, place], y_peer)
        s = i - Y_LAG
        if 0 <= s < STEPS:
            for d in range(nz):
                y_copies[s, d].wait_recv()
            core_copies[s] = send(own.at[s], oth.at[s], core_peer)
            forward(0, s)
        s = i - C_LAG
        if 0 <= s < STEPS:
            core_copies[s].wait_recv()
            forward(1, s)

    dh_load.wait()
    dh_copy.wait_recv()
    blocks = nz * ny
    tile = 256 if half % 256 == 0 else half
    for n in range(0, half, tile):
        cols = slice(n, n + tile)
        gate_value, up_value = accg[:, cols], accu[:, cols]
        first = dhv[0, :, cols].astype(jnp.float32).reshape(blocks, UNIT // 2, tile)
        second = dhv[1, :, cols].astype(jnp.float32).reshape(blocks, UNIT // 2, tile)
        upstream = jnp.stack([first, second], axis=1).reshape(blocks * UNIT, tile)
        sigmoid_gate = jax.nn.sigmoid(gate_value)
        activated = gate_value * sigmoid_gate
        hidden = (activated * up_value).reshape(blocks, 2, UNIT // 2, tile)
        for q in (0, 1):
            hst[q, :, cols] = hidden[:, q].reshape(blocks * UNIT // 2, tile).astype(jnp.bfloat16)
        dgv[:, cols] = (
            upstream * up_value * sigmoid_gate * (1.0 + gate_value * (1.0 - sigmoid_gate))
        ).astype(jnp.bfloat16)
        duv[:, cols] = (upstream * activated).astype(jnp.bfloat16)
    hid_load = load(hst.at[c], hid.at[:, mine])

    contract = (((1,), (1,)), ((), ()))

    def backward(other, s):
        return lax.dot_general(
            dgv[...], wg[other, s], contract, preferred_element_type=jnp.float32
        ) + lax.dot_general(
            duv[...], wu[other, s], contract, preferred_element_type=jnp.float32)

    core_sums, y_sums, z_sums, x_sums = {}, {}, {}, {}
    hid_copy = None
    for i in range(STEPS + Z_SUM_LAG):
        if i < STEPS:
            csend[i] = backward(1, i).astype(jnp.bfloat16)
            core_sums[i] = send(csend.at[i], crecv.at[i], core_peer)
        s = i - ADD_LAG
        if 0 <= s < STEPS:
            core_sums[s].wait_recv()
            total = crecv[s].astype(jnp.float32).reshape(blocks, UNIT, width)
            full[s % 2] = full[s % 2] + total
            for k in range(nz):
                ysend[s, k] = full[s % 2, k * ny + 1 - y].astype(jnp.bfloat16)
                keep[s, k] = full[s % 2, k * ny + y]
            y_sums[s] = send(ysend.at[s], yrecv.at[s], y_peer)
            if hid_copy is None:
                hid_copy = send(hst.at[1 - c], hid.at[:, mine], core_peer)
        if i < STEPS:
            full[i % 2] = backward(0, i).reshape(blocks, UNIT, width)
        s = i - Y_SUM_LAG
        if 0 <= s < STEPS:
            y_sums[s].wait_recv()
            for d in ring:
                zsend[s, d - 1] = (
                    keep[s, z_to[d]] + yrecv[s, z_to[d]].astype(jnp.float32)).astype(jnp.bfloat16)
                z_sums[s, d] = send(zsend.at[s, d - 1], zrecv.at[s, d - 1], z_peer[d])
            fin[s] = keep[s, z] + yrecv[s, z].astype(jnp.float32)
        s = i - Z_SUM_LAG
        if 0 <= s < STEPS:
            for d in ring:
                z_sums[s, d].wait_recv()
            done = fin[s]
            for d in ring:
                done = done + zrecv[s, d - 1].astype(jnp.float32)
            if s < half_steps:
                xsend[s] = done
                x_sums[s] = send(xsend.at[s], xrecv.at[s], x_peer)
            else:
                fin[s] = done

    for s in range(half_steps):
        cols = slice(s * width, (s + 1) * width)
        slots[x, :, cols] = fin[half_steps + s]
        x_sums[s].wait_recv()
        slots[1 - x, :, cols] = xrecv[s]

    hid_load.wait()
    hid_copy.wait_recv()
    for copy in sent:
        copy.wait_send()


def fused_body(nz, ny, tokens, expert_ids, gate_weight, up_weight, d_hidden):
    count, features = tokens.shape
    hidden_units = gate_weight.shape[1]
    rows = d_hidden.shape[0]
    width = features // (CORES * STEPS)
    half = hidden_units // CORES
    blocks = nz * ny
    half_steps = STEPS // 2
    bf, f32 = jnp.bfloat16, jnp.float32
    loads = STEPS * 5 + 2
    sends = 2 + STEPS * (nz - 1 + nz + 1) + STEPS * (2 + nz - 1) + half_steps
    hbm = pl.BlockSpec(memory_space=pl.ANY)
    vmem = pl.BlockSpec(memory_space=pltpu.VMEM)
    flops = 8 * blocks * UNIT * features * half
    ids = expert_ids.T
    staged, slots = pl.pallas_call(
        functools.partial(expert_kernel, nz, ny),
        out_shape=(
            jax.ShapeDtypeStruct((rows, hidden_units), bf),
            jax.ShapeDtypeStruct((2, UNIT, half_steps * width), f32),
        ),
        in_specs=[hbm, vmem, hbm, hbm, hbm],
        out_specs=(hbm, vmem),
        scratch_shapes=[
            pltpu.VMEM((STEPS, count, width), bf),
            pltpu.VMEM((STEPS, blocks, UNIT, width), bf),
            pltpu.VMEM((STEPS, blocks, UNIT, width), bf),
            pltpu.VMEM((2, STEPS, width, half), bf),
            pltpu.VMEM((2, STEPS, width, half), bf),
            pltpu.VMEM((blocks * UNIT, half), f32),
            pltpu.VMEM((blocks * UNIT, half), f32),
            pltpu.VMEM((2, rows, half), bf),
            pltpu.VMEM((blocks * UNIT, half), bf),
            pltpu.VMEM((blocks * UNIT, half), bf),
            pltpu.VMEM((2, rows, half), bf),
            pltpu.VMEM((STEPS, blocks * UNIT, width), bf),
            pltpu.VMEM((STEPS, blocks * UNIT, width), bf),
            pltpu.VMEM((2, blocks, UNIT, width), f32),
            pltpu.VMEM((STEPS, nz, UNIT, width), f32),
            pltpu.VMEM((STEPS, nz, UNIT, width), bf),
            pltpu.VMEM((STEPS, nz, UNIT, width), bf),
            pltpu.VMEM((STEPS, nz - 1, UNIT, width), bf),
            pltpu.VMEM((STEPS, nz - 1, UNIT, width), bf),
            pltpu.VMEM((STEPS, UNIT, width), f32),
            pltpu.VMEM((half_steps, UNIT, width), f32),
            pltpu.VMEM((half_steps, UNIT, width), f32),
            pltpu.SemaphoreType.DMA((loads,)),
            pltpu.SemaphoreType.DMA((sends,)),
            pltpu.SemaphoreType.DMA((sends,)),
        ],
        compiler_params=pltpu.CompilerParams(
            collective_id=0, has_side_effects=True, vmem_limit_bytes=56 * 1024 * 1024),
        cost_estimate=pl.CostEstimate(
            flops=flops, bytes_accessed=4 * features * half, transcendentals=0),
    )(tokens, ids, gate_weight, up_weight, d_hidden)
    d_tokens, hidden = pl.pallas_call(
        place_kernel,
        out_shape=(
            jax.ShapeDtypeStruct((count, half_steps * width), f32),
            jax.ShapeDtypeStruct((rows, hidden_units), bf),
        ),
        in_specs=[vmem, vmem, vmem],
        out_specs=(vmem, vmem),
    )(ids, slots, staged)
    return hidden, d_tokens


def split_of(mesh):
    line = mesh.devices.reshape(mesh.shape["pipe"], mesh.shape["expert"])[0]
    coords = [getattr(device, "coords", None) for device in line]
    if coords[0] is None:
        return len(line) // 2, 2
    ny = len({tuple(at)[1] for at in coords})
    return len(line) // ny, ny


def solution(mesh):
    in_specs = (
        P("expert", None),
        P("expert", None),
        P(None, "expert"),
        P(None, "expert"),
        P("pipe", "expert"),
    )
    out_specs = (P("pipe", "expert"), P("expert", "pipe"))
    nz, ny = split_of(mesh)
    fits = ny == 2 and nz > 1 and mesh.shape["pipe"] == 2 * CORES and 2 * UNIT == CAP
    body = functools.partial(fused_body, nz, ny) if fits else plain_body
    return jax.shard_map(body, mesh=mesh, in_specs=in_specs, out_specs=out_specs, check_vma=False)
```

```python
import functools

import jax
import jax.numpy as jnp
from jax import lax
from jax.experimental import pallas as pl
from jax.experimental.pallas import tpu as pltpu
from jax.sharding import PartitionSpec as P

CAP = 32
CORES = 2
UNIT = 16
STEPS = 6
Y_LAG, C_LAG = 3, 4
ADD_LAG, Y_SUM_LAG, Z_SUM_LAG = 1, 3, 6
MESH_ID = pl.DeviceIdType.MESH


def slot_select(expert_ids, first_slot, slot_count):
    is_named = jnp.any(expert_ids == 0, axis=1).astype(jnp.int32)
    slot_before = jnp.cumsum(is_named) - is_named
    positions = first_slot + jnp.arange(slot_count, dtype=jnp.int32)
    marked = (is_named[:, None] == 1) & (slot_before[:, None] == positions[None, :])
    return marked.astype(jnp.float32)


def plain_body(tokens, expert_ids, gate_weight, up_weight, d_hidden):
    hidden_units = gate_weight.shape[1]
    slot_span = CAP // lax.axis_size("pipe")
    own_select = slot_select(expert_ids, lax.axis_index("pipe") * slot_span, slot_span)
    routed = jnp.einsum(
        "tj,td->jd", own_select.astype(jnp.bfloat16), tokens, preferred_element_type=jnp.float32
    ).astype(jnp.bfloat16)
    piece = lax.all_gather(routed, "expert", axis=0, tiled=True)
    gate_part = jnp.dot(piece, gate_weight, preferred_element_type=jnp.float32)
    up_part = jnp.dot(piece, up_weight, preferred_element_type=jnp.float32)
    joined = jnp.concatenate([gate_part, up_part], axis=1)
    gate_value = joined[:, :hidden_units]
    up_value = joined[:, hidden_units:]
    sigmoid_gate = jax.nn.sigmoid(gate_value)
    activated = gate_value * sigmoid_gate
    hidden = (activated * up_value).astype(jnp.bfloat16)
    upstream = d_hidden.astype(jnp.float32)
    d_gate = (
        upstream * up_value * sigmoid_gate * (1.0 + gate_value * (1.0 - sigmoid_gate))
    ).astype(jnp.bfloat16)
    d_up = (upstream * activated).astype(jnp.bfloat16)
    result = jnp.einsum("nh,dh->nd", d_gate, gate_weight, preferred_element_type=jnp.float32)
    slot_grads = lax.psum_scatter(
        result + jnp.einsum("nh,dh->nd", d_up, up_weight, preferred_element_type=jnp.float32),
        "expert",
        scatter_dimension=0,
        tiled=True,
    )
    pieces = lax.all_to_all(slot_grads, "pipe", split_axis=1, concat_axis=0, tiled=True)
    full_select = slot_select(expert_ids, 0, CAP)
    d_tokens = jnp.einsum("tc,cd->td", full_select, pieces, precision=lax.Precision.HIGHEST)
    return (hidden, d_tokens)


def named_counts(ids, count):
    row_id = lax.broadcasted_iota(jnp.int32, (count, count), 0)
    col_id = lax.broadcasted_iota(jnp.int32, (count, count), 1)
    named_row = jnp.where((ids[0:1, :] == 0) | (ids[1:2, :] == 0), 1.0, 0.0)
    across = jnp.broadcast_to(named_row, (count, count))
    named_col = jnp.sum(jnp.where(row_id == col_id, across, 0.0), axis=1, keepdims=True)
    before_col = jnp.sum(jnp.where(col_id < row_id, across, 0.0), axis=1, keepdims=True)
    down = jnp.broadcast_to(named_col, (count, count))
    before_row = jnp.sum(jnp.where(row_id < col_id, down, 0.0), axis=0, keepdims=True)
    return named_row, before_row, named_col, before_col


def place_kernel(ids, slots, hid_in, dtok, hid_out):
    count = dtok.shape[0]
    hid_out[...] = hid_in[...]
    _, _, named_col, before_col = named_counts(ids, count)
    lane = lax.broadcasted_iota(jnp.int32, (count, 2 * UNIT), 1).astype(jnp.float32)
    placed = jnp.where((before_col == lane) & (named_col == 1.0), 1.0, 0.0)
    dtok[...] = jnp.dot(
        placed, slots[...].reshape(2 * UNIT, dtok.shape[1]),
        precision=lax.Precision.HIGHEST, preferred_element_type=jnp.float32)


def expert_kernel(nz, ny, tok, ids, gate, up, dh, hid, slots,
                  tokv, own, oth, wg, wu, accg, accu, dhv, dgv, duv, hst,
                  csend, crecv, full, keep, ysend, yrecv, zsend, zrecv, fin, xsend, xrecv,
                  load_sem, send_sem, recv_sem):
    pipe, expert = lax.axis_index("pipe"), lax.axis_index("expert")
    x, c = pipe // CORES, lax.rem(pipe, CORES)
    z, y = expert // ny, lax.rem(expert, ny)
    half_steps = STEPS // 2
    width = tokv.shape[2]
    half = wg.shape[3]
    count = tok.shape[0]
    span = width * half_steps
    ring = range(1, nz)
    z_to = {d: lax.rem(z + d, nz) for d in ring}
    z_from = {d: lax.rem(z + nz - d, nz) for d in ring}
    core_peer = (x * CORES + 1 - c, expert)
    x_peer = ((1 - x) * CORES + c, expert)
    y_peer = (pipe, z * ny + 1 - y)
    z_peer = {d: (pipe, z_to[d] * ny + y) for d in ring}

    taken = [0, 0]

    def load(src, dst):
        taken[0] += 1
        copy = pltpu.make_async_copy(src, dst, load_sem.at[taken[0] - 1])
        copy.start()
        return copy

    def send(src, dst, device):
        taken[1] += 1
        index = taken[1] - 1
        copy = pltpu.make_async_remote_copy(
            src_ref=src, dst_ref=dst, send_sem=send_sem.at[index], recv_sem=recv_sem.at[index],
            device_id=device, device_id_type=MESH_ID)
        copy.start()
        sent.append(copy)
        return copy

    sent = []

    def offset(other, s):
        part = c if other == 0 else 1 - c
        where = 1 - x if s < half_steps else x
        return pl.multiple_of((where * CORES + part) * span + (s % half_steps) * width, 128)

    barrier = pltpu.get_barrier_semaphore()
    peers = [core_peer, x_peer, y_peer] + [z_peer[d] for d in ring]
    for peer in peers:
        pl.semaphore_signal(barrier, inc=1, device_id=peer, device_id_type=MESH_ID)

    mine = pl.ds(pl.multiple_of(c * half, 128), half)
    others = pl.ds(pl.multiple_of((1 - c) * half, 128), half)
    tok_loads = [load(tok.at[:, pl.ds(offset(0, s), width)], tokv.at[s]) for s in range(STEPS)]
    w_loads = {}
    for s in range(STEPS):
        for other in (0, 1):
            rows = pl.ds(offset(other, s), width)
            w_loads[other, s] = (
                load(gate.at[rows, mine], wg.at[other, s]), load(up.at[rows, mine], wu.at[other, s]))
    dh_load = load(dh.at[:, mine], dhv.at[c])

    named_row, before_row, _, _ = named_counts(ids, count)
    slot_id = (lax.broadcasted_iota(jnp.int32, (UNIT, count), 0) + x * UNIT).astype(jnp.float32)
    select = jnp.where((before_row == slot_id) & (named_row == 1.0), 1.0, 0.0).astype(jnp.bfloat16)

    pl.semaphore_wait(barrier, len(peers))
    dh_copy = send(dh.at[:, others], dhv.at[c], core_peer)

    z_copies, y_copies, core_copies = {}, {}, {}
    for s in range(STEPS):
        tok_loads[s].wait()
        own[s, expert] = jnp.dot(
            select, tokv[s], preferred_element_type=jnp.float32).astype(jnp.bfloat16)
        for d in ring:
            z_copies[s, d] = send(own.at[s, expert], own.at[s, expert], z_peer[d])
        y_copies[s, 0] = send(own.at[s, expert], own.at[s, expert], y_peer)

    def forward(other, s):
        block = (own if other == 0 else oth)[s].reshape(nz * ny * UNIT, width)
        for copy in w_loads[other, s]:
            copy.wait()
        for acc, weight in ((accg, wg), (accu, wu)):
            term = jnp.dot(block, weight[other, s], preferred_element_type=jnp.float32)
            if other == 0 and s == 0:
                acc[...] = term
            else:
                acc[...] += term

    for i in range(STEPS + C_LAG):
        if i < STEPS:
            for d in ring:
                z_copies[i, d].wait_recv()
                place = z_from[d] * ny + y
                y_copies[i, d] = send(own.at[i, place], own.at[i, place], y_peer)
        s = i - Y_LAG
        if 0 <= s < STEPS:
            for d in range(nz):
                y_copies[s, d].wait_recv()
            core_copies[s] = send(own.at[s], oth.at[s], core_peer)
            forward(0, s)
        s = i - C_LAG
        if 0 <= s < STEPS:
            core_copies[s].wait_recv()
            forward(1, s)

    dh_load.wait()
    dh_copy.wait_recv()
    blocks = nz * ny
    tile = 256 if half % 256 == 0 else half
    for n in range(0, half, tile):
        cols = slice(n, n + tile)
        gate_value, up_value = accg[:, cols], accu[:, cols]
        first = dhv[0, :, cols].astype(jnp.float32).reshape(blocks, UNIT // 2, tile)
        second = dhv[1, :, cols].astype(jnp.float32).reshape(blocks, UNIT // 2, tile)
        upstream = jnp.stack([first, second], axis=1).reshape(blocks * UNIT, tile)
        sigmoid_gate = jax.nn.sigmoid(gate_value)
        activated = gate_value * sigmoid_gate
        hidden = (activated * up_value).reshape(blocks, 2, UNIT // 2, tile)
        for q in (0, 1):
            hst[q, :, cols] = hidden[:, q].reshape(blocks * UNIT // 2, tile).astype(jnp.bfloat16)
        dgv[:, cols] = (
            upstream * up_value * sigmoid_gate * (1.0 + gate_value * (1.0 - sigmoid_gate))
        ).astype(jnp.bfloat16)
        duv[:, cols] = (upstream * activated).astype(jnp.bfloat16)
    hid_load = load(hst.at[c], hid.at[:, mine])

    contract = (((1,), (1,)), ((), ()))

    def backward(other, s):
        return lax.dot_general(
            dgv[...], wg[other, s], contract, preferred_element_type=jnp.float32
        ) + lax.dot_general(
            duv[...], wu[other, s], contract, preferred_element_type=jnp.float32)

    core_sums, y_sums, z_sums, x_sums = {}, {}, {}, {}
    hid_copy = None
    for i in range(STEPS + Z_SUM_LAG):
        if i < STEPS:
            csend[i] = backward(1, i).astype(jnp.bfloat16)
            core_sums[i] = send(csend.at[i], crecv.at[i], core_peer)
        s = i - ADD_LAG
        if 0 <= s < STEPS:
            core_sums[s].wait_recv()
            total = crecv[s].astype(jnp.float32).reshape(blocks, UNIT, width)
            full[s % 2] = full[s % 2] + total
            for k in range(nz):
                ysend[s, k] = full[s % 2, k * ny + 1 - y].astype(jnp.bfloat16)
                keep[s, k] = full[s % 2, k * ny + y]
            y_sums[s] = send(ysend.at[s], yrecv.at[s], y_peer)
            if hid_copy is None:
                hid_copy = send(hst.at[1 - c], hid.at[:, mine], core_peer)
        if i < STEPS:
            full[i % 2] = backward(0, i).reshape(blocks, UNIT, width)
        s = i - Y_SUM_LAG
        if 0 <= s < STEPS:
            y_sums[s].wait_recv()
            for d in ring:
                zsend[s, d - 1] = (
                    keep[s, z_to[d]] + yrecv[s, z_to[d]].astype(jnp.float32)).astype(jnp.bfloat16)
                z_sums[s, d] = send(zsend.at[s, d - 1], zrecv.at[s, d - 1], z_peer[d])
            fin[s] = keep[s, z] + yrecv[s, z].astype(jnp.float32)
        s = i - Z_SUM_LAG
        if 0 <= s < STEPS:
            for d in ring:
                z_sums[s, d].wait_recv()
            done = fin[s]
            for d in ring:
                done = done + zrecv[s, d - 1].astype(jnp.float32)
            if s < half_steps:
                xsend[s] = done
                x_sums[s] = send(xsend.at[s], xrecv.at[s], x_peer)
            else:
                fin[s] = done

    for s in range(half_steps):
        cols = slice(s * width, (s + 1) * width)
        slots[x, :, cols] = fin[half_steps + s]
        x_sums[s].wait_recv()
        slots[1 - x, :, cols] = xrecv[s]

    hid_load.wait()
    hid_copy.wait_recv()
    for copy in sent:
        copy.wait_send()


def fused_body(nz, ny, tokens, expert_ids, gate_weight, up_weight, d_hidden):
    count, features = tokens.shape
    hidden_units = gate_weight.shape[1]
    rows = d_hidden.shape[0]
    width = features // (CORES * STEPS)
    half = hidden_units // CORES
    blocks = nz * ny
    half_steps = STEPS // 2
    bf, f32 = jnp.bfloat16, jnp.float32
    loads = STEPS * 5 + 2
    sends = 2 + STEPS * (nz - 1 + nz + 1) + STEPS * (2 + nz - 1) + half_steps
    hbm = pl.BlockSpec(memory_space=pl.ANY)
    vmem = pl.BlockSpec(memory_space=pltpu.VMEM)
    flops = 8 * blocks * UNIT * features * half
    ids = expert_ids.T
    staged, slots = pl.pallas_call(
        functools.partial(expert_kernel, nz, ny),
        out_shape=(
            jax.ShapeDtypeStruct((rows, hidden_units), bf),
            jax.ShapeDtypeStruct((2, UNIT, half_steps * width), f32),
        ),
        in_specs=[hbm, vmem, hbm, hbm, hbm],
        out_specs=(hbm, vmem),
        scratch_shapes=[
            pltpu.VMEM((STEPS, count, width), bf),
            pltpu.VMEM((STEPS, blocks, UNIT, width), bf),
            pltpu.VMEM((STEPS, blocks, UNIT, width), bf),
            pltpu.VMEM((2, STEPS, width, half), bf),
            pltpu.VMEM((2, STEPS, width, half), bf),
            pltpu.VMEM((blocks * UNIT, half), f32),
            pltpu.VMEM((blocks * UNIT, half), f32),
            pltpu.VMEM((2, rows, half), bf),
            pltpu.VMEM((blocks * UNIT, half), bf),
            pltpu.VMEM((blocks * UNIT, half), bf),
            pltpu.VMEM((2, rows, half), bf),
            pltpu.VMEM((STEPS, blocks * UNIT, width), bf),
            pltpu.VMEM((STEPS, blocks * UNIT, width), bf),
            pltpu.VMEM((2, blocks, UNIT, width), f32),
            pltpu.VMEM((STEPS, nz, UNIT, width), f32),
            pltpu.VMEM((STEPS, nz, UNIT, width), bf),
            pltpu.VMEM((STEPS, nz, UNIT, width), bf),
            pltpu.VMEM((STEPS, nz - 1, UNIT, width), bf),
            pltpu.VMEM((STEPS, nz - 1, UNIT, width), bf),
            pltpu.VMEM((STEPS, UNIT, width), f32),
            pltpu.VMEM((half_steps, UNIT, width), f32),
            pltpu.VMEM((half_steps, UNIT, width), f32),
            pltpu.SemaphoreType.DMA((loads,)),
            pltpu.SemaphoreType.DMA((sends,)),
            pltpu.SemaphoreType.DMA((sends,)),
        ],
        compiler_params=pltpu.CompilerParams(
            collective_id=0, has_side_effects=True, vmem_limit_bytes=56 * 1024 * 1024),
        cost_estimate=pl.CostEstimate(
            flops=flops, bytes_accessed=4 * features * half, transcendentals=0),
    )(tokens, ids, gate_weight, up_weight, d_hidden)
    d_tokens, hidden = pl.pallas_call(
        place_kernel,
        out_shape=(
            jax.ShapeDtypeStruct((count, half_steps * width), f32),
            jax.ShapeDtypeStruct((rows, hidden_units), bf),
        ),
        in_specs=[vmem, vmem, vmem],
        out_specs=(vmem, vmem),
    )(ids, slots, staged)
    return hidden, d_tokens


def split_of(mesh):
    line = mesh.devices.reshape(mesh.shape["pipe"], mesh.shape["expert"])[0]
    coords = [getattr(device, "coords", None) for device in line]
    if coords[0] is None:
        return len(line) // 2, 2
    ny = len({tuple(at)[1] for at in coords})
    return len(line) // ny, ny


def solution(mesh):
    in_specs = (
        P("expert", None),
        P("expert", None),
        P(None, "expert"),
        P(None, "expert"),
        P("pipe", "expert"),
    )
    out_specs = (P("pipe", "expert"), P("expert", "pipe"))
    nz, ny = split_of(mesh)
    fits = ny == 2 and nz > 1 and mesh.shape["pipe"] == 2 * CORES and 2 * UNIT == CAP
    body = functools.partial(fused_body, nz, ny) if fits else plain_body
    return jax.shard_map(body, mesh=mesh, in_specs=in_specs, out_specs=out_specs, check_vma=False)
```
